256 devices in a mesh: row: 32 (over x_lo, z, core), col: 8 (over x_hi, y).
Axes of the slice: x: 4 (x_hi: 2, x_lo: 2; x = x_hi * 2 + x_lo), y: 4, z: 8, core: 2. Of those that a mesh axis runs over, the one named last changes fastest.
Arguments:
- rhs: float32 [2031616], P(('row', 'col')), may hold values from -6 to 6
- blocks: float32 [32, 8, 64, 128, 128], P('row', 'col'), may hold values from -0.5 to 0.5
- blk_row: int32 [32, 8, 64], P('row', 'col'), may hold values from 0 to 495
- blk_col: int32 [32, 8, 64], P('row', 'col'), may hold values from 0 to 511
Outputs:
- solution: float32 [524288], P(('col', 'row'))
- rel_residual: float32 [], replicated
The draws below stay inside these ranges and needn't reach their ends.
Inputs may be any that keep to these rules, and one draw needn't show every extreme that they name: `blk_row`: each device holds 64 blocks; blocks listed twice at the same place are added.
All inputs are finite; a program needn't handle non-finite values.
Results may differ from the reference program's by a relative error of at most 0.00013.
Values sent between devices are 32-bit elements; how exact they have to be, the bound alone decides.
A program may use at most 64 MiB of HBM per device.

```python
import jax
import jax.numpy as jnp
from jax import lax

BLK = 128
ROWB_DEV = 496
COLB_DEV = 512
NB_DEV = 64
ITERS = 3
ROWS = 2031616
N_ROW = 32
N_COL = 8


def set_ends(entries, key, low, top_value):
    dims = entries.shape
    place = [jax.random.randint(jax.random.fold_in(key, axis), (), 0, dims[axis]) for axis in range(len(dims))]
    entries = entries.at[tuple(place)].set(low)
    longest = dims.index(max(dims))
    place[longest] = (place[longest] + 1) % dims[longest]
    return entries.at[tuple(place)].set(top_value)


def block_scale(stream_key, dims, cuts, least, high):
    factor_of = 1.0
    for dim, blocks in cuts:
        steps = jax.random.uniform(jax.random.fold_in(jax.random.fold_in(stream_key, 6), dim), (blocks,), jnp.float32, least / len(cuts), high / len(cuts))
        factor_of = factor_of * jnp.repeat(jnp.exp(steps), dims[dim] // blocks).reshape((-1,) + (1,) * (len(dims) - 1 - dim))
    return factor_of


def scatter_about(stream_key, dims, width, limit, pieces=(), held_as=jnp.bfloat16):
    array = jax.random.normal(stream_key, dims, jnp.float32) * width
    if len(pieces) > 0:
        array = block_scale(stream_key, dims, pieces, -0.22, 0.18) * array
    return jnp.clip(array, min=-limit, max=limit).astype(held_as)


def setup_inputs(seed: int = 0) -> dict:
    keys = jax.random.split(jax.random.key(seed), 5)
    return {
        "rhs": scatter_about(keys[0], (ROWS,), 1.0, 6.0, ((0, 256),), jnp.float32),
        "blocks": scatter_about(keys[1], (N_ROW, N_COL, NB_DEV, BLK, BLK), BLK ** -0.5, 0.5, ((0, 32), (1, 8)), jnp.float32),
        "blk_row": set_ends(jax.random.randint(keys[2], (N_ROW, N_COL, NB_DEV), 0, ROWB_DEV), jax.random.fold_in(keys[2], 1), 0, ROWB_DEV - 1).astype(jnp.int32),
        "blk_col": set_ends(jax.random.randint(keys[3], (N_ROW, N_COL, NB_DEV), 0, COLB_DEV), jax.random.fold_in(keys[3], 1), 0, COLB_DEV - 1).astype(jnp.int32),
    }


def forward(blocks, blk_row, blk_col, vec):
    parts = vec.reshape(N_COL, COLB_DEV, BLK)
    col_index = jnp.arange(N_COL, dtype=jnp.int32)[None, :, None]
    picked = parts[col_index, blk_col]
    prod = jnp.einsum('rcnij,rcnj->rcni', blocks, picked, precision=lax.Precision.HIGHEST)
    rows = jnp.arange(N_ROW, dtype=jnp.int32)[:, None, None] * ROWB_DEV + blk_row
    total = jnp.zeros((N_ROW * ROWB_DEV, BLK), jnp.float32).at[rows].add(prod)
    return total.reshape(N_ROW * ROWB_DEV * BLK)

def backward(blocks, blk_row, blk_col, vec):
    parts = vec.reshape(N_ROW, ROWB_DEV, BLK)
    row_index = jnp.arange(N_ROW, dtype=jnp.int32)[:, None, None]
    picked = parts[row_index, blk_row]
    prod = jnp.einsum('rcnij,rcni->rcnj', blocks, picked, precision=lax.Precision.HIGHEST)
    cols = jnp.arange(N_COL, dtype=jnp.int32)[None, :, None] * COLB_DEV + blk_col
    total = jnp.zeros((N_COL * COLB_DEV, BLK), jnp.float32).at[cols].add(prod)
    return total.reshape(N_COL * COLB_DEV * BLK)

def reference(rhs, blocks, blk_row, blk_col):
    beta_first = jnp.sqrt(jnp.sum(rhs * rhs))
    u = rhs / beta_first
    v_raw = backward(blocks, blk_row, blk_col, u)
    alpha = jnp.sqrt(jnp.sum(v_raw * v_raw))
    v = v_raw / alpha
    w = v
    solution = jnp.zeros_like(v)
    phibar = beta_first
    rhobar = alpha
    for step in range(ITERS):
        u_raw = forward(blocks, blk_row, blk_col, v) - alpha * u
        beta = jnp.sqrt(jnp.sum(u_raw * u_raw))
        u = u_raw / beta
        v_raw = backward(blocks, blk_row, blk_col, u) - beta * v
        alpha = jnp.sqrt(jnp.sum(v_raw * v_raw))
        v = v_raw / alpha
        rho = jnp.sqrt(rhobar * rhobar + beta * beta)
        cosine = rhobar / rho
        sine = beta / rho
        theta = sine * alpha
        rhobar = -cosine * alpha
        phi = cosine * phibar
        phibar = sine * phibar
        solution = solution + phi / rho * w
        w = v - theta / rho * w
    return (solution, phibar / beta_first)
```

```python
import functools

import jax
import jax.numpy as jnp
from jax import lax
from jax.experimental import pallas as pl
from jax.experimental.pallas import tpu as pltpu
from jax.sharding import PartitionSpec as P

BLK = 128
NB = 64
ITERS = 3
N_COL = 8
N_CHIP = 16
PER_COL = 62
MESH = pl.DeviceIdType.MESH
F32 = jnp.float32
BF16 = jnp.bfloat16
MSG = NB + 1
PIECE = 17
UNROLL = 8


def split3(x):
    hi = x.astype(BF16)
    rest = x - hi.astype(F32)
    mid = rest.astype(BF16)
    low = (rest - mid.astype(F32)).astype(BF16)
    return hi, mid, low


def total_of(x):
    return jnp.broadcast_to(jnp.sum(jnp.sum(x, axis=0, keepdims=True), axis=1, keepdims=True), (1, BLK))


def kernel(rows_at, cols_at, rhs, index, blocks_hbm, sol_out, rel_out,
           blocks, u, v, v_old, put_rows, put_cols, parts,
           col_src, col_dst, core_src, core_dst, rs_src, rs_dst, vb, ids, fin_src, fin_dst, w, sol,
           blk_sem, col_send, col_recv, core_send, core_recv, rs_send, rs_recv, ag_send, ag_recv,
           half_send, half_recv, ids_send, ids_recv, fin_send, fin_recv, finc_send, finc_recv, fin_core):
    r = lax.axis_index("row")
    c = lax.axis_index("col")
    q = r // 2
    h = lax.rem(r, 2)
    other = q * 2 + (1 - h)
    partner = {"row": other, "col": c}

    load = pltpu.make_async_copy(blocks_hbm, blocks, blk_sem)
    load.start()

    def col_peer(d):
        return {"row": r, "col": lax.rem(c + d, N_COL)}

    def chip_of(d):
        return lax.rem(q + d, N_CHIP)

    barrier = pltpu.get_barrier_semaphore()
    for d in range(1, N_COL):
        pl.semaphore_signal(barrier, inc=1, device_id=col_peer(d), device_id_type=MESH)
    for d in range(1, N_CHIP):
        pl.semaphore_signal(barrier, inc=1, device_id={"row": chip_of(d) * 2 + h, "col": c}, device_id_type=MESH)
    pl.semaphore_signal(barrier, inc=1, device_id=partner, device_id_type=MESH)

    col_src[0, 0:PER_COL, :] = rhs[...]
    col_src[0, PER_COL:NB, :] = jnp.zeros((NB - PER_COL, BLK), F32)
    col_src[0, NB:MSG, :] = index[...]
    pl.semaphore_wait(barrier, N_COL - 1 + N_CHIP - 1 + 1)

    def col_start(k):
        for d in range(1, N_COL):
            pltpu.make_async_remote_copy(
                src_ref=col_src.at[k], dst_ref=col_dst.at[k, c], send_sem=col_send.at[k], recv_sem=col_recv.at[k],
                device_id=col_peer(d), device_id_type=MESH).start()

    def col_wait(k):
        pltpu.make_async_copy(col_dst.at[k, pl.ds(0, N_COL - 1)], col_dst.at[k, pl.ds(0, N_COL - 1)], col_recv.at[k]).wait()

    ids_copy = pltpu.make_async_remote_copy(
        src_ref=index, dst_ref=ids, send_sem=ids_send, recv_sem=ids_recv, device_id=partner, device_id_type=MESH)
    col_start(0)
    ids_copy.start()

    sub = lax.broadcasted_iota(jnp.int32, (BLK, BLK), 0)
    lane = lax.broadcasted_iota(jnp.int32, (BLK, BLK), 1)
    eye = sub == lane
    lane1 = lax.broadcasted_iota(jnp.int32, (1, BLK), 1)
    low_half = lane1 < NB

    v_old[...] = jnp.zeros((512, BLK), F32)
    w[...] = jnp.zeros((16, BLK), F32)
    sol[...] = jnp.zeros((16, BLK), F32)
    col_dst[0, c] = col_src[0]

    ids_copy.wait()
    mine = index[...]
    theirs = ids[...]
    first = jnp.where(h == 0, mine, theirs)
    second = jnp.where(h == 0, theirs, mine)
    pair_cols = jnp.where(low_half, pltpu.roll(first, NB, 1), second)
    i256 = lax.broadcasted_iota(jnp.int32, (256, BLK), 0)
    owner_block = ((i256 // 16) * 32 + h * 16 + lax.rem(i256, 16)).astype(F32)
    put_cols[...] = jnp.where(owner_block == pair_cols, 1.0, 0.0).astype(BF16)

    col_wait(0)
    i512 = lax.broadcasted_iota(jnp.int32, (512, BLK), 0).astype(F32)
    for j in range(N_COL // 2):
        a = col_dst[0, 2 * j, NB:MSG, :]
        b = col_dst[0, 2 * j + 1, NB:MSG, :]
        pair = jnp.where(low_half, a, pltpu.roll(b, NB, 1))
        put_rows[:, j * BLK:(j + 1) * BLK] = jnp.where(i512 == pair, 1.0, 0.0).astype(BF16)
    for j in range(N_COL):
        u[j * NB:(j + 1) * NB, :] = col_dst[0, j, 0:NB, :]
    load.wait()

    def step(k, carry):
        rhobar, phibar, beta_first = carry
        su = total_of(u[...] * u[...])

        def back(g, _):
            for t in range(UNROLL):
                n = g * UNROLL + t
                row = u[pl.ds(rows_at[n], 1), :]
                column = jnp.sum(jnp.where(eye, row, 0.0), axis=1, keepdims=True)
                core_src[k, pl.ds(n, 1), :] = jnp.sum(blocks[n] * column, axis=0, keepdims=True)
            return 0
        lax.fori_loop(0, NB // UNROLL, back, 0)
        core_src[k, NB:MSG, :] = su
        swap = pltpu.make_async_remote_copy(
            src_ref=core_src.at[k], dst_ref=core_dst.at[k], send_sem=core_send.at[k], recv_sem=core_recv.at[k],
            device_id=partner, device_id_type=MESH)
        swap.start()
        for p, x in enumerate(split3(core_src[k, 0:NB, :])):
            parts[pl.ds(pl.multiple_of(h * NB, NB), NB), p * BLK:(p + 1) * BLK] = x
        swap.wait_recv()
        for p, x in enumerate(split3(core_dst[k, 0:NB, :])):
            parts[pl.ds(pl.multiple_of((1 - h) * NB, NB), NB), p * BLK:(p + 1) * BLK] = x
        dense = jnp.dot(put_cols[...], parts[0:2 * NB, :], preferred_element_type=F32)
        dense = dense[:, 0:BLK] + dense[:, BLK:2 * BLK] + dense[:, 2 * BLK:3 * BLK]
        both = su + core_dst[k, NB:MSG, :]
        for j in range(N_CHIP):
            rs_src[k, j, 0:16, :] = dense[j * 16:(j + 1) * 16, :]
            rs_src[k, j, 16:PIECE, :] = both
        for d in range(1, N_CHIP):
            there = chip_of(d)
            pltpu.make_async_remote_copy(
                src_ref=rs_src.at[k, there], dst_ref=rs_dst.at[k, q], send_sem=rs_send.at[k], recv_sem=rs_recv.at[k],
                device_id={"row": there * 2 + h, "col": c}, device_id_type=MESH).start()
        rs_dst[k, q] = rs_src[k, q]
        pltpu.make_async_copy(rs_dst.at[k, pl.ds(0, N_CHIP - 1)], rs_dst.at[k, pl.ds(0, N_CHIP - 1)], rs_recv.at[k]).wait()
        piece = rs_dst[k, 0]
        for j in range(1, N_CHIP):
            piece = piece + rs_dst[k, j]
        vb[k, q, h] = piece[0:16, :]
        for d in range(1, N_CHIP):
            pltpu.make_async_remote_copy(
                src_ref=vb.at[k, q, h], dst_ref=vb.at[k, q, h], send_sem=ag_send.at[k], recv_sem=ag_recv.at[k],
                device_id={"row": chip_of(d) * 2 + h, "col": c}, device_id_type=MESH).start()
        beta = jnp.sqrt(piece[16:17, :])
        u[...] = u[...] / beta
        beta_first = jnp.where(k == 0, beta, beta_first)
        pltpu.make_async_copy(vb.at[k, pl.ds(0, N_CHIP - 1), h], vb.at[k, pl.ds(0, N_CHIP - 1), h], ag_recv.at[k]).wait()
        give = pltpu.make_async_remote_copy(
            src_ref=vb.at[k, :, h], dst_ref=vb.at[k, :, h], send_sem=half_send.at[k], recv_sem=half_recv.at[k],
            device_id=partner, device_id_type=MESH)
        give.start()
        give.wait_recv()
        v[...] = vb[k].reshape(512, BLK) / beta - beta * v_old[...]
        sv = total_of(v[...] * v[...])

        def front(g, _):
            for t in range(UNROLL):
                n = g * UNROLL + t
                row = v[pl.ds(cols_at[n], 1), :]
                column = jnp.sum(blocks[n] * row, axis=1, keepdims=True)
                col_src[k + 1, pl.ds(n, 1), :] = jnp.sum(jnp.where(eye, column, 0.0), axis=0, keepdims=True)
            return 0
        lax.fori_loop(0, NB // UNROLL, front, 0)
        col_src[k + 1, NB:MSG, :] = sv
        col_start(k + 1)
        col_dst[k + 1, c] = col_src[k + 1]
        col_wait(k + 1)
        square = col_dst[k + 1, 0, NB:MSG, :]
        for j in range(1, N_COL):
            square = square + col_dst[k + 1, j, NB:MSG, :]
        alpha = jnp.sqrt(square)
        for j in range(N_COL):
            for p, x in enumerate(split3(col_dst[k + 1, j, 0:NB, :])):
                parts[j * NB:(j + 1) * NB, p * BLK:(p + 1) * BLK] = x
        front_sum = jnp.dot(put_rows[...], parts[...], preferred_element_type=F32)
        front_sum = front_sum[:, 0:BLK] + front_sum[:, BLK:2 * BLK] + front_sum[:, 2 * BLK:3 * BLK]
        u[...] = front_sum / alpha - alpha * u[...]
        v_old[...] = v[...] / alpha

        unit = v_old[pl.ds(pl.multiple_of(r * 16, 16), 16), :]
        rho = jnp.sqrt(rhobar * rhobar + beta * beta)
        cosine = rhobar / rho
        sine = beta / rho
        theta = sine * alpha
        phi = cosine * phibar
        w_now = w[...]
        sol[...] = sol[...] + phi / rho * w_now
        w[...] = unit - theta / rho * w_now
        rhobar = jnp.where(k == 0, alpha, -cosine * alpha)
        phibar = jnp.where(k == 0, beta, sine * phibar)
        return rhobar, phibar, beta_first

    one = jnp.ones((1, BLK), F32)
    rhobar, phibar, beta_first = lax.fori_loop(0, ITERS, step, (one, jnp.zeros((1, BLK), F32), one))

    su = total_of(u[...] * u[...])
    fin_src[0] = jnp.broadcast_to(su, (8, BLK))
    swap = pltpu.make_async_remote_copy(
        src_ref=fin_src.at[0], dst_ref=fin_core, send_sem=finc_send, recv_sem=finc_recv,
        device_id=partner, device_id_type=MESH)
    swap.start()
    swap.wait_recv()
    both = fin_src[0] + fin_core[...]
    fin_src[1] = both
    for d in range(1, N_CHIP):
        pltpu.make_async_remote_copy(
            src_ref=fin_src.at[1], dst_ref=fin_dst.at[q], send_sem=fin_send, recv_sem=fin_recv,
            device_id={"row": chip_of(d) * 2 + h, "col": c}, device_id_type=MESH).start()
    fin_dst[q] = both
    pltpu.make_async_copy(fin_dst.at[pl.ds(0, N_CHIP - 1)], fin_dst.at[pl.ds(0, N_CHIP - 1)], fin_recv).wait()
    square = fin_dst[0]
    for j in range(1, N_CHIP):
        square = square + fin_dst[j]
    beta = jnp.sqrt(square[0:1, :])
    rho = jnp.sqrt(rhobar * rhobar + beta * beta)
    phi = rhobar / rho * phibar
    sol_out[...] = sol[...] + phi / rho * w[...]
    rel_out[...] = jnp.broadcast_to(beta / rho * phibar / beta_first, (8, BLK))

    swap.wait_send()
    ids_wait = pltpu.make_async_copy(fin_dst.at[pl.ds(0, N_CHIP - 1)], fin_dst.at[pl.ds(0, N_CHIP - 1)], fin_send)
    ids_wait.wait()

    def drain_col(k, _):
        pltpu.make_async_copy(col_dst.at[k, pl.ds(0, N_COL - 1)], col_dst.at[k, pl.ds(0, N_COL - 1)], col_send.at[k]).wait()
        return 0
    lax.fori_loop(0, ITERS + 1, drain_col, 0)

    def drain_row(k, _):
        pltpu.make_async_copy(core_dst.at[k], core_dst.at[k], core_send.at[k]).wait()
        pltpu.make_async_copy(rs_dst.at[k, pl.ds(0, N_CHIP - 1)], rs_dst.at[k, pl.ds(0, N_CHIP - 1)], rs_send.at[k]).wait()
        pltpu.make_async_copy(vb.at[k, pl.ds(0, N_CHIP - 1), h], vb.at[k, pl.ds(0, N_CHIP - 1), h], ag_send.at[k]).wait()
        pltpu.make_async_copy(vb.at[k, :, h], vb.at[k, :, h], half_send.at[k]).wait()
        return 0
    lax.fori_loop(0, ITERS, drain_row, 0)


def on_device(rhs, blocks, blk_row, blk_col):
    rows = blk_row.reshape(NB)
    rows = rows // PER_COL * NB + rows % PER_COL
    cols = blk_col.reshape(NB)
    index = jnp.concatenate([rows, cols]).astype(F32).reshape(1, BLK)
    vmem = pl.BlockSpec(memory_space=pltpu.VMEM)
    smem = pl.BlockSpec(memory_space=pltpu.SMEM)
    dma = pltpu.SemaphoreType.DMA
    sol, rel = pl.pallas_call(
        kernel,
        out_shape=(jax.ShapeDtypeStruct((16, BLK), F32), jax.ShapeDtypeStruct((8, BLK), F32)),
        in_specs=[smem, smem, vmem, vmem, pl.BlockSpec(memory_space=pl.ANY)],
        out_specs=(vmem, vmem),
        scratch_shapes=[
            pltpu.VMEM((NB, BLK, BLK), F32),
            pltpu.VMEM((512, BLK), F32),
            pltpu.VMEM((512, BLK), F32),
            pltpu.VMEM((512, BLK), F32),
            pltpu.VMEM((512, 512), BF16),
            pltpu.VMEM((256, BLK), BF16),
            pltpu.VMEM((512, 3 * BLK), BF16),
            pltpu.VMEM((ITERS + 1, MSG, BLK), F32),
            pltpu.VMEM((ITERS + 1, N_COL, MSG, BLK), F32),
            pltpu.VMEM((ITERS, MSG, BLK), F32),
            pltpu.VMEM((ITERS, MSG, BLK), F32),
            pltpu.VMEM((ITERS, N_CHIP, PIECE, BLK), F32),
            pltpu.VMEM((ITERS, N_CHIP, PIECE, BLK), F32),
            pltpu.VMEM((ITERS, N_CHIP, 2, 16, BLK), F32),
            pltpu.VMEM((1, BLK), F32),
            pltpu.VMEM((2, 8, BLK), F32),
            pltpu.VMEM((N_CHIP, 8, BLK), F32),
            pltpu.VMEM((16, BLK), F32),
            pltpu.VMEM((16, BLK), F32),
            dma, dma((ITERS + 1,)), dma((ITERS + 1,)), dma((ITERS,)), dma((ITERS,)), dma((ITERS,)), dma((ITERS,)),
            dma((ITERS,)), dma((ITERS,)), dma((ITERS,)), dma((ITERS,)), dma, dma, dma, dma, dma, dma,
            pltpu.VMEM((8, BLK), F32),
        ],
        compiler_params=pltpu.CompilerParams(
            collective_id=0, has_side_effects=True, vmem_limit_bytes=48 * 1024 * 1024),
    )(rows, cols, rhs.reshape(PER_COL, BLK), index, blocks.reshape(NB, BLK, BLK))
    return sol.reshape(16 * BLK), rel[0, 0]


def solution(mesh):
    return jax.shard_map(
        on_device,
        mesh=mesh,
        in_specs=(
            P(("row", "col")),
            P("row", "col", None, None, None),
            P("row", "col", None),
            P("row", "col", None),
        ),
        out_specs=(P(("col", "row")), P()),
        check_vma=False,
    )
```

```python
import jax
import jax.numpy as jnp
from jax import lax
from jax.experimental import pallas as pl
from jax.experimental.pallas import tpu as pltpu
from jax.sharding import PartitionSpec as P

BLK = 128
NB = 64
ITERS = 3
N_ROW = 32
N_COL = 8
N_CHIP = 16
ROWB = 496
COLB = 512
PER_COL = 62
MESH = pl.DeviceIdType.MESH
F32 = jnp.float32
BF16 = jnp.bfloat16
MSG = NB + 1
PIECE = 17
UNROLL = 8


def ring(d, n):
    return min(d % n, n - d % n)


CHIPS = sorted(((x, z) for x in range(2) for z in range(8) if (x, z) != (0, 0)), key=lambda t: -(t[0] + ring(t[1], 8)))
CORES = sorted(
    ((x, z, s) for x in range(2) for z in range(8) for s in range(2) if (x, z, s) != (0, 0, 0)),
    key=lambda t: -(t[0] + ring(t[1], 8) + 0.1 * t[2]))
COLS = sorted(((x, y) for x in range(2) for y in range(4) if (x, y) != (0, 0)), key=lambda t: -(4 * t[0] + ring(t[1], 4)))


def split3(x):
    hi = x.astype(BF16)
    rest = x - hi.astype(F32)
    mid = rest.astype(BF16)
    low = (rest - mid.astype(F32)).astype(BF16)
    return hi, mid, low


def join3(x):
    return x[:, 0:BLK] + x[:, BLK:2 * BLK] + x[:, 2 * BLK:3 * BLK]


def total_of(x):
    return jnp.broadcast_to(jnp.sum(jnp.sum(x, axis=0, keepdims=True), axis=1, keepdims=True), (1, BLK))


def kernel(rows_hbm, cols_hbm, rhs_hbm, blocks_hbm, sol_out, rel_out,
           raw, tiles, u, v, picks, spread, sums, put_rows, put_cols, parts, parts2,
           col_src, col_dst, core_src, core_dst, rs_src, rs_dst, vb, ids_src, ids_dst, fin_src, fin_dst, w, sol, start,
           rows_v, cols_v, rows_at, cols_at,
           load_sem, col_send, near_recv, far_recv, core_send, core_recv, rs_send, rs_recv, ag_send, ag_recv,
           half_send, half_recv, ids_send, ids_recv, fin_send, fin_recv):
    r = lax.axis_index("row")
    c = lax.axis_index("col")
    q = r // 2
    h = lax.rem(r, 2)
    x_low = q // 8
    z = lax.rem(q, 8)
    side = c // 4
    y = lax.rem(c, 4)
    partner = {"row": q * 2 + (1 - h), "col": c}

    def chip_at(dx, dz):
        return lax.rem(x_low + dx, 2) * 8 + lax.rem(z + dz, 8)

    def row_peer(dx, dz, dh):
        return {"row": chip_at(dx, dz) * 2 + lax.rem(h + dh, 2), "col": c}

    def col_peer(dx, dy):
        return {"row": r, "col": lax.rem(side + dx, 2) * 4 + lax.rem(y + dy, 4)}

    barrier = pltpu.get_barrier_semaphore()
    for d in CORES:
        pl.semaphore_signal(barrier, inc=1, device_id=row_peer(*d), device_id_type=MESH)
    for d in COLS:
        pl.semaphore_signal(barrier, inc=1, device_id=col_peer(*d), device_id_type=MESH)

    loads = [
        pltpu.make_async_copy(rows_hbm, rows_v, load_sem.at[0]),
        pltpu.make_async_copy(cols_hbm, cols_v, load_sem.at[1]),
        pltpu.make_async_copy(rhs_hbm, col_src.at[0, pl.ds(0, PER_COL)], load_sem.at[2]),
        pltpu.make_async_copy(rows_hbm, rows_at, load_sem.at[3]),
        pltpu.make_async_copy(cols_hbm, cols_at, load_sem.at[4]),
        pltpu.make_async_copy(blocks_hbm, raw, load_sem.at[5]),
    ]
    for copy in loads:
        copy.start()
    col_src[0, PER_COL:MSG, :] = jnp.zeros((MSG - PER_COL, BLK), F32)
    ids_src[...] = jnp.zeros((1, BLK), F32)
    loads[0].wait()
    loads[1].wait()
    col_src[0, NB:MSG, 0:NB] = rows_v[...].astype(F32)
    ids_src[:, 0:NB] = cols_v[...].astype(F32)
    loads[2].wait()
    pl.semaphore_wait(barrier, len(CORES) + len(COLS))

    def col_start(k):
        for d in COLS:
            pltpu.make_async_remote_copy(
                src_ref=col_src.at[k], dst_ref=col_dst.at[k, c], send_sem=col_send.at[k],
                recv_sem=(far_recv if d[0] else near_recv).at[k],
                device_id=col_peer(*d), device_id_type=MESH).start()

    def wait_bytes(ref, sem):
        pltpu.make_async_copy(ref, ref, sem).wait()

    ids_copy = pltpu.make_async_remote_copy(
        src_ref=ids_src, dst_ref=ids_dst, send_sem=ids_send, recv_sem=ids_recv, device_id=partner, device_id_type=MESH)
    col_start(0)
    ids_copy.start()

    lane1 = lax.broadcasted_iota(jnp.int32, (1, BLK), 1)
    low_half = lane1 < NB

    v[...] = jnp.zeros((COLB, BLK), F32)
    start[0:1, :] = jnp.ones((1, BLK), F32)
    start[1:2, :] = jnp.zeros((1, BLK), F32)
    w[...] = jnp.zeros((16, BLK), F32)
    sol[...] = jnp.zeros((16, BLK), F32)
    col_dst[0, c] = col_src[0]
    loads[3].wait()
    loads[4].wait()
    loads[5].wait()

    def arrange(g, _):
        for t in range(2):
            i = g * 2 + t
            top = raw[pl.ds(i, NB, stride=BLK), :]
            low = raw[pl.ds(NB + i, NB, stride=BLK), :]
            tiles[i] = jnp.concatenate([top, low], axis=0).T
        return 0
    lax.fori_loop(0, NB // 2, arrange, 0)

    ids_copy.wait_recv()
    mine = ids_src[...]
    theirs = ids_dst[...]
    first = jnp.where(h == 0, mine, theirs)
    second = jnp.where(h == 0, theirs, mine)
    pair_cols = jnp.where(low_half, first, pltpu.roll(second, NB, 1))
    i256 = lax.broadcasted_iota(jnp.int32, (256, BLK), 0)
    owner_block = ((i256 // 16) * 32 + h * 16 + lax.rem(i256, 16)).astype(F32)
    put_cols[...] = jnp.where(owner_block == pair_cols, 1.0, 0.0).astype(BF16)

    wait_bytes(col_dst.at[0, pl.ds(0, 3)], near_recv.at[0])
    wait_bytes(col_dst.at[0, pl.ds(0, 4)], far_recv.at[0])
    for j in range(N_COL):
        u[j * PER_COL:(j + 1) * PER_COL, :] = col_dst[0, j, 0:PER_COL, :]
    row_number = lax.broadcasted_iota(jnp.int32, (ROWB, BLK), 0).astype(F32)

    def make_put_rows():
        for j in range(N_COL // 2):
            a = col_dst[0, 2 * j, NB:MSG, :]
            b = col_dst[0, 2 * j + 1, NB:MSG, :]
            pair = jnp.where(low_half, a, pltpu.roll(b, NB, 1))
            put_rows[j // 2, :, (j % 2) * BLK:(j % 2 + 1) * BLK] = jnp.where(row_number == pair, 1.0, 0.0).astype(BF16)

    def lsqr(k, rhobar, phibar, alpha, beta):
        unit = v[pl.ds(pl.multiple_of(r * 16, 16), 16), :] / alpha
        rho = jnp.sqrt(rhobar * rhobar + beta * beta)
        cosine = rhobar / rho
        sine = beta / rho
        theta = sine * alpha
        phi = cosine * phibar
        w_now = w[...]
        sol[...] = sol[...] + phi / rho * w_now
        w[...] = unit - theta / rho * w_now
        return jnp.where(k == 1, alpha, -cosine * alpha), jnp.where(k == 1, beta, sine * phibar)

    def step(k, carry):
        rhobar, phibar, beta_first, alpha_old, beta_old = carry
        su = total_of(u[...] * u[...])
        for n in range(NB):
            picks[n:n + 1, :] = u[pl.ds(rows_at[0, n], 1), :]
        chosen = picks[...]
        spread[...] = jnp.concatenate([chosen, pltpu.roll(chosen, NB, 1)], axis=0).T[0:NB, :]

        def back(g, acc):
            for t in range(UNROLL):
                i = g * UNROLL + t
                acc = acc + tiles[i] * spread[pl.ds(i, 1), :]
            return acc
        acc = lax.fori_loop(0, NB // UNROLL, back, jnp.zeros((BLK, BLK), F32)).T
        core_src[k, 0:NB, :] = acc[0:NB, :] + acc[NB:BLK, :]
        core_src[k, NB:MSG, :] = su
        swap = pltpu.make_async_remote_copy(
            src_ref=core_src.at[k], dst_ref=core_dst.at[k], send_sem=core_send.at[k], recv_sem=core_recv.at[k],
            device_id=partner, device_id_type=MESH)
        swap.start()
        for p, x in enumerate(split3(core_src[k, 0:NB, :])):
            parts2[pl.ds(pl.multiple_of(h * NB, NB), NB), p * BLK:(p + 1) * BLK] = x
        swap.wait_recv()
        for p, x in enumerate(split3(core_dst[k, 0:NB, :])):
            parts2[pl.ds(pl.multiple_of((1 - h) * NB, NB), NB), p * BLK:(p + 1) * BLK] = x
        dense = join3(jnp.dot(put_cols[...], parts2[...], preferred_element_type=F32))
        both = su + core_dst[k, NB:MSG, :]
        for j in range(N_CHIP):
            rs_src[k, j, 0:16, :] = dense[j * 16:(j + 1) * 16, :]
            rs_src[k, j, 16:PIECE, :] = both
        for d in CHIPS:
            pltpu.make_async_remote_copy(
                src_ref=rs_src.at[k, chip_at(*d)], dst_ref=rs_dst.at[k, q], send_sem=rs_send.at[k], recv_sem=rs_recv.at[k],
                device_id=row_peer(*d, 0), device_id_type=MESH).start()
        rs_dst[k, q] = rs_src[k, q]
        rhobar, phibar = lsqr(k, rhobar, phibar, alpha_old, beta_old)
        v[...] = v[...] * (1.0 / alpha_old)

        @pl.when(k == 0)
        def _():
            make_put_rows()
        wait_bytes(rs_dst.at[k, pl.ds(0, N_CHIP - 1)], rs_recv.at[k])
        piece = rs_dst[k, 0]
        for j in range(1, N_CHIP):
            piece = piece + rs_dst[k, j]
        vb[k, q, h] = piece[0:16, :]
        for d in CHIPS:
            pltpu.make_async_remote_copy(
                src_ref=vb.at[k, q, h], dst_ref=vb.at[k, q, h], send_sem=ag_send.at[k], recv_sem=ag_recv.at[k],
                device_id=row_peer(*d, 0), device_id_type=MESH).start()
        beta = jnp.sqrt(piece[16:17, :])
        inv_beta = 1.0 / beta
        u[...] = u[...] * inv_beta
        beta_first = jnp.where(k == 0, beta, beta_first)
        wait_bytes(vb.at[k, pl.ds(0, N_CHIP - 1), h], ag_recv.at[k])
        give = pltpu.make_async_remote_copy(
            src_ref=vb.at[k, :, h], dst_ref=vb.at[k, :, h], send_sem=half_send.at[k], recv_sem=half_recv.at[k],
            device_id=partner, device_id_type=MESH)
        give.start()

        def half_v(s):
            squares = jnp.zeros((16, BLK), F32)
            for j in range(N_CHIP):
                at = pl.ds(pl.multiple_of(j * 32 + s * 16, 16), 16)
                x = vb[k, j, s] * inv_beta - beta * v[at, :]
                v[at, :] = x
                squares = squares + x * x
            return total_of(squares)
        sv = half_v(h)
        give.wait_recv()
        sv = sv + half_v(1 - h)

        for n in range(NB):
            picks[n:n + 1, :] = v[pl.ds(cols_at[0, n], 1), :]
        chosen = picks[...]
        x = jnp.concatenate([chosen, chosen], axis=0).T

        def front(g, _):
            for t in range(UNROLL):
                i = g * UNROLL + t
                sums[pl.ds(pl.multiple_of(i * 8, 8), 8), :] = jnp.sum((tiles[i] * x).reshape(16, 8, BLK), axis=0)
            return 0
        lax.fori_loop(0, NB // UNROLL, front, 0)
        rows = sums[pl.ds(0, NB, stride=8), :]
        for s in range(1, 8):
            rows = rows + sums[pl.ds(s, NB, stride=8), :]
        rows = jnp.concatenate([rows, rows], axis=0).T
        col_src[k + 1, 0:NB, :] = jnp.where(low_half, rows[0:NB, :], rows[NB:BLK, :])
        col_src[k + 1, NB:MSG, :] = sv
        col_start(k + 1)
        col_dst[k + 1, c] = col_src[k + 1]

        def scatter(g):
            for j in range(4):
                for p, x in enumerate(split3(col_dst[k + 1, g * 4 + j, 0:NB, :])):
                    parts[g, j * NB:(j + 1) * NB, p * BLK:(p + 1) * BLK] = x
            return join3(jnp.dot(put_rows[g], parts[g], preferred_element_type=F32))
        wait_bytes(col_dst.at[k + 1, pl.ds(0, 3)], near_recv.at[k + 1])
        near = scatter(side)
        wait_bytes(col_dst.at[k + 1, pl.ds(0, 4)], far_recv.at[k + 1])
        far = scatter(1 - side)
        square = col_dst[k + 1, 0, NB:MSG, :]
        for j in range(1, N_COL):
            square = square + col_dst[k + 1, j, NB:MSG, :]
        alpha = jnp.sqrt(square)
        u[...] = (near + far) * (1.0 / alpha) - alpha * u[...]
        return rhobar, phibar, beta_first, alpha, beta

    one = start[0:1, :]
    rhobar, phibar, beta_first, alpha, beta = lax.fori_loop(0, ITERS, step, (one, start[1:2, :], one, one, one))

    su = total_of(u[...] * u[...])
    fin_src[...] = su
    for d in CORES:
        pltpu.make_async_remote_copy(
            src_ref=fin_src, dst_ref=fin_dst.at[r], send_sem=fin_send, recv_sem=fin_recv,
            device_id=row_peer(*d), device_id_type=MESH).start()
    fin_dst[r] = su
    rhobar, phibar = lsqr(ITERS, rhobar, phibar, alpha, beta)
    last = fin_dst.at[pl.ds(0, N_ROW - 1)]

    def drain(k, _):
        wait_bytes(core_dst.at[k], core_send.at[k])
        wait_bytes(rs_dst.at[k, pl.ds(0, N_CHIP - 1)], rs_send.at[k])
        wait_bytes(vb.at[k, pl.ds(0, N_CHIP - 1), h], ag_send.at[k])
        wait_bytes(vb.at[k, :, h], half_send.at[k])
        wait_bytes(col_dst.at[k, pl.ds(0, N_COL - 1)], col_send.at[k])
        return 0
    lax.fori_loop(0, ITERS, drain, 0)
    wait_bytes(col_dst.at[ITERS, pl.ds(0, N_COL - 1)], col_send.at[ITERS])
    ids_copy.wait_send()

    wait_bytes(last, fin_recv)
    square = fin_dst[0]
    for j in range(1, N_ROW):
        square = square + fin_dst[j]
    beta = jnp.sqrt(square)
    rho = jnp.sqrt(rhobar * rhobar + beta * beta)
    phi = rhobar / rho * phibar
    sol_out[...] = sol[...] + phi / rho * w[...]
    rel_out[...] = jnp.broadcast_to(beta / rho * phibar / beta_first, (8, BLK))
    wait_bytes(last, fin_send)


def on_device(rhs, blocks, blk_row, blk_col):
    vmem = pl.BlockSpec(memory_space=pltpu.VMEM)
    hbm = pl.BlockSpec(memory_space=pl.ANY)
    dma = pltpu.SemaphoreType.DMA
    many = dma((ITERS + 1,))
    sol, rel = pl.pallas_call(
        kernel,
        out_shape=(jax.ShapeDtypeStruct((16, BLK), F32), jax.ShapeDtypeStruct((8, BLK), F32)),
        in_specs=[hbm, hbm, hbm, hbm],
        out_specs=(vmem, vmem),
        scratch_shapes=[
            pltpu.VMEM((NB * BLK, BLK), F32),
            pltpu.VMEM((NB, BLK, BLK), F32),
            pltpu.VMEM((ROWB, BLK), F32),
            pltpu.VMEM((COLB, BLK), F32),
            pltpu.VMEM((NB, BLK), F32),
            pltpu.VMEM((NB, BLK), F32),
            pltpu.VMEM((NB * 8, BLK), F32),
            pltpu.VMEM((2, ROWB, 256), BF16),
            pltpu.VMEM((256, BLK), BF16),
            pltpu.VMEM((2, 256, 3 * BLK), BF16),
            pltpu.VMEM((2 * NB, 3 * BLK), BF16),
            pltpu.VMEM((ITERS + 1, MSG, BLK), F32),
            pltpu.VMEM((ITERS + 1, N_COL, MSG, BLK), F32),
            pltpu.VMEM((ITERS, MSG, BLK), F32),
            pltpu.VMEM((ITERS, MSG, BLK), F32),
            pltpu.VMEM((ITERS, N_CHIP, PIECE, BLK), F32),
            pltpu.VMEM((ITERS, N_CHIP, PIECE, BLK), F32),
            pltpu.VMEM((ITERS, N_CHIP, 2, 16, BLK), F32),
            pltpu.VMEM((1, BLK), F32),
            pltpu.VMEM((1, BLK), F32),
            pltpu.VMEM((1, BLK), F32),
            pltpu.VMEM((N_ROW, 1, BLK), F32),
            pltpu.VMEM((16, BLK), F32),
            pltpu.VMEM((16, BLK), F32),
            pltpu.VMEM((8, BLK), F32),
            pltpu.VMEM((1, NB), jnp.int32),
            pltpu.VMEM((1, NB), jnp.int32),
            pltpu.SMEM((1, NB), jnp.int32),
            pltpu.SMEM((1, NB), jnp.int32),
            dma((6,)), many, many, many, many, many, many, many, many, many, many, many, dma, dma, dma, dma,
        ],
        compiler_params=pltpu.CompilerParams(
            collective_id=0, has_side_effects=True, vmem_limit_bytes=60 * 1024 * 1024),
    )(blk_row.reshape(1, NB), blk_col.reshape(1, NB), rhs.reshape(PER_COL, BLK), blocks.reshape(NB * BLK, BLK))
    return sol.reshape(16 * BLK), rel[0, 0]


def solution(mesh):
    return jax.shard_map(
        on_device,
        mesh=mesh,
        in_specs=(
            P(("row", "col")),
            P("row", "col", None, None, None),
            P("row", "col", None),
            P("row", "col", None),
        ),
        out_specs=(P(("col", "row")), P()),
        check_vma=False,
    )
```

```python
import jax
import jax.numpy as jnp
from jax import lax
from jax.experimental import pallas as pl
from jax.experimental.pallas import tpu as pltpu
from jax.sharding import PartitionSpec as P

BLK = 128
NB = 64
ITERS = 3
N_ROW = 32
N_COL = 8
N_CHIP = 16
ROWB = 496
COLB = 512
PER_COL = 62
MESH = pl.DeviceIdType.MESH
F32 = jnp.float32
BF16 = jnp.bfloat16
MSG = NB + 1
PIECE = 17
UNROLL = 8


def ring(d, n):
    return min(d % n, n - d % n)


CHIPS = sorted(((x, z) for x in range(2) for z in range(8) if (x, z) != (0, 0)), key=lambda t: -(t[0] + ring(t[1], 8)))
CORES = sorted(
    ((x, z, s) for x in range(2) for z in range(8) for s in range(2) if (x, z, s) != (0, 0, 0)),
    key=lambda t: -(t[0] + ring(t[1], 8) + 0.1 * t[2]))
COLS = sorted(((x, y) for x in range(2) for y in range(4) if (x, y) != (0, 0)), key=lambda t: -(4 * t[0] + ring(t[1], 4)))


def split3(x):
    hi = x.astype(BF16)
    rest = x - hi.astype(F32)
    mid = rest.astype(BF16)
    low = (rest - mid.astype(F32)).astype(BF16)
    return hi, mid, low


def join3(x):
    return x[:, 0:BLK] + x[:, BLK:2 * BLK] + x[:, 2 * BLK:3 * BLK]


def total_of(x):
    return jnp.broadcast_to(jnp.sum(jnp.sum(x, axis=0, keepdims=True), axis=1, keepdims=True), (1, BLK))


def kernel(rows_hbm, cols_hbm, rhs_hbm, blocks_hbm, sol_out, rel_out,
           raw, tiles, u, v, picks, spread, sums, put_rows, put_cols, parts, parts2,
           col_src, col_dst, core_src, core_dst, rs_src, rs_dst, vb, ids_src, ids_dst, fin_src, fin_dst, w, sol, start,
           rows_v, cols_v, rows_at, cols_at,
           load_sem, col_send, near_recv, far_recv, core_send, core_recv, rs_send, rs_recv, ag_send, ag_recv,
           half_send, half_recv, ids_send, ids_recv, fin_send, fin_recv):
    r = lax.axis_index("row")
    c = lax.axis_index("col")
    q = r // 2
    h = lax.rem(r, 2)
    x_low = q // 8
    z = lax.rem(q, 8)
    side = c // 4
    y = lax.rem(c, 4)
    partner = {"row": q * 2 + (1 - h), "col": c}

    def chip_at(dx, dz):
        return lax.rem(x_low + dx, 2) * 8 + lax.rem(z + dz, 8)

    def row_peer(dx, dz, dh):
        return {"row": chip_at(dx, dz) * 2 + lax.rem(h + dh, 2), "col": c}

    def col_peer(dx, dy):
        return {"row": r, "col": lax.rem(side + dx, 2) * 4 + lax.rem(y + dy, 4)}

    barrier = pltpu.get_barrier_semaphore()
    for d in CORES:
        pl.semaphore_signal(barrier, inc=1, device_id=row_peer(*d), device_id_type=MESH)
    for d in COLS:
        pl.semaphore_signal(barrier, inc=1, device_id=col_peer(*d), device_id_type=MESH)

    loads = [
        pltpu.make_async_copy(rows_hbm, rows_v, load_sem.at[0]),
        pltpu.make_async_copy(cols_hbm, cols_v, load_sem.at[1]),
        pltpu.make_async_copy(rhs_hbm, col_src.at[0, pl.ds(0, PER_COL)], load_sem.at[2]),
        pltpu.make_async_copy(rows_hbm, rows_at, load_sem.at[3]),
        pltpu.make_async_copy(cols_hbm, cols_at, load_sem.at[4]),
        pltpu.make_async_copy(blocks_hbm, raw, load_sem.at[5]),
    ]
    for copy in loads:
        copy.start()
    col_src[0, PER_COL:MSG, :] = jnp.zeros((MSG - PER_COL, BLK), F32)
    ids_src[...] = jnp.zeros((1, BLK), F32)
    loads[0].wait()
    loads[1].wait()
    col_src[0, NB:MSG, 0:NB] = rows_v[...].astype(F32)
    ids_src[:, 0:NB] = cols_v[...].astype(F32)
    loads[2].wait()
    pl.semaphore_wait(barrier, len(CORES) + len(COLS))

    def col_start(k):
        for d in COLS:
            pltpu.make_async_remote_copy(
                src_ref=col_src.at[k], dst_ref=col_dst.at[k, c], send_sem=col_send.at[k],
                recv_sem=(far_recv if d[0] else near_recv).at[k],
                device_id=col_peer(*d), device_id_type=MESH).start()

    def wait_bytes(ref, sem):
        pltpu.make_async_copy(ref, ref, sem).wait()

    ids_copy = pltpu.make_async_remote_copy(
        src_ref=ids_src, dst_ref=ids_dst, send_sem=ids_send, recv_sem=ids_recv, device_id=partner, device_id_type=MESH)
    col_start(0)
    ids_copy.start()

    lane1 = lax.broadcasted_iota(jnp.int32, (1, BLK), 1)
    low_half = lane1 < NB

    v[...] = jnp.zeros((COLB, BLK), F32)
    start[0:1, :] = jnp.ones((1, BLK), F32)
    start[1:2, :] = jnp.zeros((1, BLK), F32)
    w[...] = jnp.zeros((16, BLK), F32)
    sol[...] = jnp.zeros((16, BLK), F32)
    col_dst[0, c] = col_src[0]
    loads[3].wait()
    loads[4].wait()
    loads[5].wait()

    def arrange(g, _):
        for t in range(2):
            i = g * 2 + t
            top = raw[pl.ds(i, NB, stride=BLK), :]
            low = raw[pl.ds(NB + i, NB, stride=BLK), :]
            tiles[i] = jnp.concatenate([top, low], axis=0).T
        return 0
    lax.fori_loop(0, NB // 2, arrange, 0)

    ids_copy.wait_recv()
    mine = ids_src[...]
    theirs = ids_dst[...]
    first = jnp.where(h == 0, mine, theirs)
    second = jnp.where(h == 0, theirs, mine)
    pair_cols = jnp.where(low_half, first, pltpu.roll(second, NB, 1))
    i256 = lax.broadcasted_iota(jnp.int32, (256, BLK), 0)
    owner_block = ((i256 // 16) * 32 + h * 16 + lax.rem(i256, 16)).astype(F32)
    put_cols[...] = jnp.where(owner_block == pair_cols, 1.0, 0.0).astype(BF16)

    wait_bytes(col_dst.at[0, pl.ds(0, 3)], near_recv.at[0])
    wait_bytes(col_dst.at[0, pl.ds(0, 4)], far_recv.at[0])
    for j in range(N_COL):
        u[j * PER_COL:(j + 1) * PER_COL, :] = col_dst[0, j, 0:PER_COL, :]
    row_number = lax.broadcasted_iota(jnp.int32, (ROWB, BLK), 0).astype(F32)

    def make_put_rows():
        for j in range(N_COL // 2):
            a = col_dst[0, 2 * j, NB:MSG, :]
            b = col_dst[0, 2 * j + 1, NB:MSG, :]
            pair = jnp.where(low_half, a, pltpu.roll(b, NB, 1))
            put_rows[j // 2, :, (j % 2) * BLK:(j % 2 + 1) * BLK] = jnp.where(row_number == pair, 1.0, 0.0).astype(BF16)

    def lsqr(k, rhobar, phibar, alpha, beta):
        unit = v[pl.ds(pl.multiple_of(r * 16, 16), 16), :] / alpha
        rho = jnp.sqrt(rhobar * rhobar + beta * beta)
        cosine = rhobar / rho
        sine = beta / rho
        theta = sine * alpha
        phi = cosine * phibar
        w_now = w[...]
        sol[...] = sol[...] + phi / rho * w_now
        w[...] = unit - theta / rho * w_now
        return jnp.where(k == 1, alpha, -cosine * alpha), jnp.where(k == 1, beta, sine * phibar)

    def step(k, carry):
        rhobar, phibar, beta_first, alpha_old, beta_old = carry
        su = total_of(u[...] * u[...])
        for n in range(NB):
            picks[n:n + 1, :] = u[pl.ds(rows_at[0, n], 1), :]
        chosen = picks[...]
        spread[...] = jnp.concatenate([chosen, pltpu.roll(chosen, NB, 1)], axis=0).T[0:NB, :]

        def back(g, acc):
            for t in range(UNROLL):
                i = g * UNROLL + t
                acc = acc + tiles[i] * spread[pl.ds(i, 1), :]
            return acc
        acc = lax.fori_loop(0, NB // UNROLL, back, jnp.zeros((BLK, BLK), F32)).T
        core_src[k, 0:NB, :] = acc[0:NB, :] + acc[NB:BLK, :]
        core_src[k, NB:MSG, :] = su
        swap = pltpu.make_async_remote_copy(
            src_ref=core_src.at[k], dst_ref=core_dst.at[k], send_sem=core_send.at[k], recv_sem=core_recv.at[k],
            device_id=partner, device_id_type=MESH)
        swap.start()
        for p, x in enumerate(split3(core_src[k, 0:NB, :])):
            parts2[pl.ds(pl.multiple_of(h * NB, NB), NB), p * BLK:(p + 1) * BLK] = x
        swap.wait_recv()
        for p, x in enumerate(split3(core_dst[k, 0:NB, :])):
            parts2[pl.ds(pl.multiple_of((1 - h) * NB, NB), NB), p * BLK:(p + 1) * BLK] = x
        dense = join3(jnp.dot(put_cols[...], parts2[...], preferred_element_type=F32))
        both = su + core_dst[k, NB:MSG, :]
        for j in range(N_CHIP):
            rs_src[k, j, 0:16, :] = dense[j * 16:(j + 1) * 16, :]
            rs_src[k, j, 16:PIECE, :] = both
        for d in CHIPS:
            pltpu.make_async_remote_copy(
                src_ref=rs_src.at[k, chip_at(*d)], dst_ref=rs_dst.at[k, q], send_sem=rs_send.at[k], recv_sem=rs_recv.at[k],
                device_id=row_peer(*d, 0), device_id_type=MESH).start()
        rs_dst[k, q] = rs_src[k, q]
        rhobar, phibar = lsqr(k, rhobar, phibar, alpha_old, beta_old)
        v[...] = v[...] * (1.0 / alpha_old)

        @pl.when(k == 0)
        def _():
            make_put_rows()
        wait_bytes(rs_dst.at[k, pl.ds(0, N_CHIP - 1)], rs_recv.at[k])
        piece = rs_dst[k, 0]
        for j in range(1, N_CHIP):
            piece = piece + rs_dst[k, j]
        vb[k, q, h] = piece[0:16, :]
        for d in CHIPS:
            pltpu.make_async_remote_copy(
                src_ref=vb.at[k, q, h], dst_ref=vb.at[k, q, h], send_sem=ag_send.at[k], recv_sem=ag_recv.at[k],
                device_id=row_peer(*d, 0), device_id_type=MESH).start()
        beta = jnp.sqrt(piece[16:17, :])
        inv_beta = 1.0 / beta
        u[...] = u[...] * inv_beta
        beta_first = jnp.where(k == 0, beta, beta_first)
        wait_bytes(vb.at[k, pl.ds(0, N_CHIP - 1), h], ag_recv.at[k])
        give = pltpu.make_async_remote_copy(
            src_ref=vb.at[k, :, h], dst_ref=vb.at[k, :, h], send_sem=half_send.at[k], recv_sem=half_recv.at[k],
            device_id=partner, device_id_type=MESH)
        give.start()

        def half_v(s):
            squares = jnp.zeros((16, BLK), F32)
            for j in range(N_CHIP):
                at = pl.ds(pl.multiple_of(j * 32 + s * 16, 16), 16)
                x = vb[k, j, s] * inv_beta - beta * v[at, :]
                v[at, :] = x
                squares = squares + x * x
            return total_of(squares)
        sv = half_v(h)
        give.wait_recv()
        sv = sv + half_v(1 - h)

        for n in range(NB):
            picks[n:n + 1, :] = v[pl.ds(cols_at[0, n], 1), :]
        chosen = picks[...]
        x = jnp.concatenate([chosen, chosen], axis=0).T

        def front(g, _):
            for t in range(UNROLL):
                i = g * UNROLL + t
                sums[pl.ds(pl.multiple_of(i * 8, 8), 8), :] = jnp.sum((tiles[i] * x).reshape(16, 8, BLK), axis=0)
            return 0
        lax.fori_loop(0, NB // UNROLL, front, 0)
        rows = sums[pl.ds(0, NB, stride=8), :]
        for s in range(1, 8):
            rows = rows + sums[pl.ds(s, NB, stride=8), :]
        rows = jnp.concatenate([rows, rows], axis=0).T
        col_src[k + 1, 0:NB, :] = jnp.where(low_half, rows[0:NB, :], rows[NB:BLK, :])
        col_src[k + 1, NB:MSG, :] = sv
        col_start(k + 1)
        col_dst[k + 1, c] = col_src[k + 1]

        def scatter(g):
            for j in range(4):
                for p, x in enumerate(split3(col_dst[k + 1, g * 4 + j, 0:NB, :])):
                    parts[g, j * NB:(j + 1) * NB, p * BLK:(p + 1) * BLK] = x
            return join3(jnp.dot(put_rows[g], parts[g], preferred_element_type=F32))
        wait_bytes(col_dst.at[k + 1, pl.ds(0, 3)], near_recv.at[k + 1])
        near = scatter(side)
        wait_bytes(col_dst.at[k + 1, pl.ds(0, 4)], far_recv.at[k + 1])
        far = scatter(1 - side)
        square = col_dst[k + 1, 0, NB:MSG, :]
        for j in range(1, N_COL):
            square = square + col_dst[k + 1, j, NB:MSG, :]
        alpha = jnp.sqrt(square)
        u[...] = (near + far) * (1.0 / alpha) - alpha * u[...]
        return rhobar, phibar, beta_first, alpha, beta

    one = start[0:1, :]
    rhobar, phibar, beta_first, alpha, beta = lax.fori_loop(0, ITERS, step, (one, start[1:2, :], one, one, one))

    su = total_of(u[...] * u[...])
    fin_src[...] = su
    for d in CORES:
        pltpu.make_async_remote_copy(
            src_ref=fin_src, dst_ref=fin_dst.at[r], send_sem=fin_send, recv_sem=fin_recv,
            device_id=row_peer(*d), device_id_type=MESH).start()
    fin_dst[r] = su
    rhobar, phibar = lsqr(ITERS, rhobar, phibar, alpha, beta)
    last = fin_dst.at[pl.ds(0, N_ROW - 1)]

    def drain(k, _):
        wait_bytes(core_dst.at[k], core_send.at[k])
        wait_bytes(rs_dst.at[k, pl.ds(0, N_CHIP - 1)], rs_send.at[k])
        wait_bytes(vb.at[k, pl.ds(0, N_CHIP - 1), h], ag_send.at[k])
        wait_bytes(vb.at[k, :, h], half_send.at[k])
        wait_bytes(col_dst.at[k, pl.ds(0, N_COL - 1)], col_send.at[k])
        return 0
    lax.fori_loop(0, ITERS, drain, 0)
    wait_bytes(col_dst.at[ITERS, pl.ds(0, N_COL - 1)], col_send.at[ITERS])
    ids_copy.wait_send()

    wait_bytes(last, fin_recv)
    square = fin_dst[0]
    for j in range(1, N_ROW):
        square = square + fin_dst[j]
    beta = jnp.sqrt(square)
    rho = jnp.sqrt(rhobar * rhobar + beta * beta)
    phi = rhobar / rho * phibar
    sol_out[...] = sol[...] + phi / rho * w[...]
    rel_out[...] = jnp.broadcast_to(beta / rho * phibar / beta_first, (8, BLK))
    wait_bytes(last, fin_send)


def on_device(rhs, blocks, blk_row, blk_col):
    vmem = pl.BlockSpec(memory_space=pltpu.VMEM)
    hbm = pl.BlockSpec(memory_space=pl.ANY)
    dma = pltpu.SemaphoreType.DMA
    many = dma((ITERS + 1,))
    sol, rel = pl.pallas_call(
        kernel,
        out_shape=(pltpu.VMEM((16, BLK), F32), pltpu.VMEM((8, BLK), F32)),
        in_specs=[hbm, hbm, hbm, hbm],
        out_specs=(vmem, vmem),
        scratch_shapes=[
            pltpu.VMEM((NB * BLK, BLK), F32),
            pltpu.VMEM((NB, BLK, BLK), F32),
            pltpu.VMEM((ROWB, BLK), F32),
            pltpu.VMEM((COLB, BLK), F32),
            pltpu.VMEM((NB, BLK), F32),
            pltpu.VMEM((NB, BLK), F32),
            pltpu.VMEM((NB * 8, BLK), F32),
            pltpu.VMEM((2, ROWB, 256), BF16),
            pltpu.VMEM((256, BLK), BF16),
            pltpu.VMEM((2, 256, 3 * BLK), BF16),
            pltpu.VMEM((2 * NB, 3 * BLK), BF16),
            pltpu.VMEM((ITERS + 1, MSG, BLK), F32),
            pltpu.VMEM((ITERS + 1, N_COL, MSG, BLK), F32),
            pltpu.VMEM((ITERS, MSG, BLK), F32),
            pltpu.VMEM((ITERS, MSG, BLK), F32),
            pltpu.VMEM((ITERS, N_CHIP, PIECE, BLK), F32),
            pltpu.VMEM((ITERS, N_CHIP, PIECE, BLK), F32),
            pltpu.VMEM((ITERS, N_CHIP, 2, 16, BLK), F32),
            pltpu.VMEM((1, BLK), F32),
            pltpu.VMEM((1, BLK), F32),
            pltpu.VMEM((1, BLK), F32),
            pltpu.VMEM((N_ROW, 1, BLK), F32),
            pltpu.VMEM((16, BLK), F32),
            pltpu.VMEM((16, BLK), F32),
            pltpu.VMEM((8, BLK), F32),
            pltpu.VMEM((1, NB), jnp.int32),
            pltpu.VMEM((1, NB), jnp.int32),
            pltpu.SMEM((1, NB), jnp.int32),
            pltpu.SMEM((1, NB), jnp.int32),
            dma((6,)), many, many, many, many, many, many, many, many, many, many, many, dma, dma, dma, dma,
        ],
        compiler_params=pltpu.CompilerParams(
            collective_id=0, has_side_effects=True, vmem_limit_bytes=60 * 1024 * 1024),
    )(blk_row.reshape(1, NB), blk_col.reshape(1, NB), rhs.reshape(PER_COL, BLK), blocks.reshape(NB * BLK, BLK))
    return sol.reshape(16 * BLK), rel[0, 0]


def solution(mesh):
    return jax.shard_map(
        on_device,
        mesh=mesh,
        in_specs=(
            P(("row", "col")),
            P("row", "col", None, None, None),
            P("row", "col", None),
            P("row", "col", None),
        ),
        out_specs=(P(("col", "row")), P()),
        check_vma=False,
    )
```

```python
import jax
import jax.numpy as jnp
from jax import lax
from jax.experimental import pallas as pl
from jax.experimental.pallas import tpu as pltpu
from jax.sharding import PartitionSpec as P

BLK = 128
NB = 64
ITERS = 3
N_ROW = 32
N_COL = 8
N_CHIP = 16
ROWB = 496
COLB = 512
PER_COL = 62
MESH = pl.DeviceIdType.MESH
F32 = jnp.float32
BF16 = jnp.bfloat16
MSG = NB + 1
PIECE = 17
UNROLL = 32


def ring(d, n):
    return min(d % n, n - d % n)


CHIPS = sorted(((x, z) for x in range(2) for z in range(8) if (x, z) != (0, 0)), key=lambda t: -(t[0] + ring(t[1], 8)))
CORES = sorted(
    ((x, z, s) for x in range(2) for z in range(8) for s in range(2) if (x, z, s) != (0, 0, 0)),
    key=lambda t: -(t[0] + ring(t[1], 8) + 0.1 * t[2]))
COLS = sorted(((x, y) for x in range(2) for y in range(4) if (x, y) != (0, 0)), key=lambda t: -(4 * t[0] + ring(t[1], 4)))


def split3(x):
    hi = x.astype(BF16)
    rest = x - hi.astype(F32)
    mid = rest.astype(BF16)
    low = (rest - mid.astype(F32)).astype(BF16)
    return hi, mid, low


def join3(x):
    return x[:, 0:BLK] + x[:, BLK:2 * BLK] + x[:, 2 * BLK:3 * BLK]


def total_of(x):
    return jnp.broadcast_to(jnp.sum(jnp.sum(x, axis=0, keepdims=True), axis=1, keepdims=True), (1, BLK))


def kernel(rows_hbm, cols_hbm, rhs_hbm, blocks_hbm, sol_out, rel_out,
           raw, tiles, u, v, picks, u_picks, near_sum, spread, sums, put_rows, pick_rows, put_cols, parts, parts2,
           col_src, col_dst, core_src, core_dst, rs_src, rs_dst, half_src, half_dst, vb, ids_src, ids_dst, fin_src, fin_dst, w, sol, start,
           rows_v, cols_v, rows_at, cols_at,
           load_sem, col_send, near_recv, far_recv, core_send, core_recv, rs_send, rs_recv, ag_send, ag_recv,
           norm_send, norm_recv, half_send, half_recv, ids_send, ids_recv, fin_send, fin_recv):
    r = lax.axis_index("row")
    c = lax.axis_index("col")
    q = r // 2
    h = lax.rem(r, 2)
    x_low = q // 8
    z = lax.rem(q, 8)
    side = c // 4
    y = lax.rem(c, 4)
    partner = {"row": q * 2 + (1 - h), "col": c}

    def chip_at(dx, dz):
        return lax.rem(x_low + dx, 2) * 8 + lax.rem(z + dz, 8)

    def row_peer(dx, dz, dh):
        return {"row": chip_at(dx, dz) * 2 + lax.rem(h + dh, 2), "col": c}

    def col_peer(dx, dy):
        return {"row": r, "col": lax.rem(side + dx, 2) * 4 + lax.rem(y + dy, 4)}

    barrier = pltpu.get_barrier_semaphore()
    for d in CORES:
        pl.semaphore_signal(barrier, inc=1, device_id=row_peer(*d), device_id_type=MESH)
    for d in COLS:
        pl.semaphore_signal(barrier, inc=1, device_id=col_peer(*d), device_id_type=MESH)

    loads = [
        pltpu.make_async_copy(rows_hbm, rows_v, load_sem.at[0]),
        pltpu.make_async_copy(cols_hbm, cols_v, load_sem.at[1]),
        pltpu.make_async_copy(rhs_hbm, col_src.at[0, pl.ds(0, PER_COL)], load_sem.at[2]),
        pltpu.make_async_copy(rows_hbm, rows_at, load_sem.at[3]),
        pltpu.make_async_copy(cols_hbm, cols_at, load_sem.at[4]),
        pltpu.make_async_copy(blocks_hbm, raw, load_sem.at[5]),
    ]
    for copy in loads:
        copy.start()
    col_src[0, PER_COL:MSG, :] = jnp.zeros((MSG - PER_COL, BLK), F32)
    ids_src[...] = jnp.zeros((1, BLK), F32)
    loads[0].wait()
    loads[1].wait()
    col_src[0, NB:MSG, 0:NB] = rows_v[...].astype(F32)
    ids_src[:, 0:NB] = cols_v[...].astype(F32)
    loads[2].wait()
    pl.semaphore_wait(barrier, len(CORES) + len(COLS))

    def col_start(k):
        for d in COLS:
            pltpu.make_async_remote_copy(
                src_ref=col_src.at[k], dst_ref=col_dst.at[k, c], send_sem=col_send.at[k],
                recv_sem=(far_recv if d[0] else near_recv).at[k],
                device_id=col_peer(*d), device_id_type=MESH).start()

    def wait_bytes(ref, sem):
        pltpu.make_async_copy(ref, ref, sem).wait()

    ids_copy = pltpu.make_async_remote_copy(
        src_ref=ids_src, dst_ref=ids_dst, send_sem=ids_send, recv_sem=ids_recv, device_id=partner, device_id_type=MESH)
    col_start(0)
    ids_copy.start()

    lane1 = lax.broadcasted_iota(jnp.int32, (1, BLK), 1)
    low_half = lane1 < NB

    v[...] = jnp.zeros((COLB, BLK), F32)
    start[0:1, :] = jnp.ones((1, BLK), F32)
    start[1:2, :] = jnp.zeros((1, BLK), F32)
    w[...] = jnp.zeros((16, BLK), F32)
    sol[...] = jnp.zeros((16, BLK), F32)
    col_dst[0, c] = col_src[0]
    loads[3].wait()
    loads[4].wait()
    loads[5].wait()

    def arrange(g, _):
        for t in range(2):
            i = g * 2 + t
            top = raw[pl.ds(i, NB, stride=BLK), :]
            low = raw[pl.ds(NB + i, NB, stride=BLK), :]
            tiles[i] = jnp.concatenate([top, low], axis=0).T
        return 0
    lax.fori_loop(0, NB // 2, arrange, 0)

    ids_copy.wait_recv()
    mine = ids_src[...]
    theirs = ids_dst[...]
    first = jnp.where(h == 0, mine, theirs)
    second = jnp.where(h == 0, theirs, mine)
    pair_cols = jnp.where(low_half, first, pltpu.roll(second, NB, 1))
    i256 = lax.broadcasted_iota(jnp.int32, (256, BLK), 0)
    owner_block = ((i256 // 16) * 32 + h * 16 + lax.rem(i256, 16)).astype(F32)
    put_cols[...] = jnp.where(owner_block == pair_cols, 1.0, 0.0).astype(BF16)

    wait_bytes(col_dst.at[0, pl.ds(0, 3)], near_recv.at[0])
    wait_bytes(col_dst.at[0, pl.ds(0, 4)], far_recv.at[0])
    for j in range(N_COL):
        u[j * PER_COL:(j + 1) * PER_COL, :] = col_dst[0, j, 0:PER_COL, :]
    row_number = lax.broadcasted_iota(jnp.int32, (ROWB, BLK), 0).astype(F32)

    def make_put_rows():
        own_rows = jnp.broadcast_to(col_src[0, NB:MSG, :], (BLK, BLK)).T[0:NB, :]
        for j in range(N_COL // 2):
            a = col_dst[0, 2 * j, NB:MSG, :]
            b = col_dst[0, 2 * j + 1, NB:MSG, :]
            pair = jnp.where(low_half, a, pltpu.roll(b, NB, 1))
            lanes = slice((j % 2) * BLK, (j % 2 + 1) * BLK)
            put_rows[j // 2, :, lanes] = jnp.where(row_number == pair, 1.0, 0.0).astype(BF16)
            pick_rows[j // 2, :, lanes] = jnp.where(own_rows == pair, 1.0, 0.0).astype(BF16)

    def lsqr(k, rhobar, phibar, alpha, beta):
        unit = v[pl.ds(pl.multiple_of(r * 16, 16), 16), :] / alpha
        rho = jnp.sqrt(rhobar * rhobar + beta * beta)
        cosine = rhobar / rho
        sine = beta / rho
        theta = sine * alpha
        phi = cosine * phibar
        w_now = w[...]
        sol[...] = sol[...] + phi / rho * w_now
        w[...] = unit - theta / rho * w_now
        return jnp.where(k == 1, alpha, -cosine * alpha), jnp.where(k == 1, beta, sine * phibar)

    for n in range(NB):
        u_picks[n:n + 1, :] = u[pl.ds(rows_at[0, n], 1), :]

    def finish_u(alpha):
        far = join3(jnp.dot(put_rows[1 - side], parts[1 - side], preferred_element_type=F32))
        u[...] = (near_sum[...] + far) * (1.0 / alpha) - alpha * u[...]

    def step(k, carry):
        rhobar, phibar, beta_first, alpha_old, beta_old = carry
        chosen = u_picks[...]
        spread[...] = jnp.concatenate([chosen, pltpu.roll(chosen, NB, 1)], axis=0).T[0:NB, :]

        def back(g, acc):
            for t in range(UNROLL):
                i = g * UNROLL + t
                acc = acc + tiles[i] * spread[pl.ds(i, 1), :]
            return acc
        acc = lax.fori_loop(0, NB // UNROLL, back, jnp.zeros((BLK, BLK), F32)).T
        core_src[k] = acc[0:NB, :] + acc[NB:BLK, :]
        swap = pltpu.make_async_remote_copy(
            src_ref=core_src.at[k], dst_ref=core_dst.at[k], send_sem=core_send.at[k], recv_sem=core_recv.at[k],
            device_id=partner, device_id_type=MESH)
        swap.start()
        for p, x in enumerate(split3(core_src[k])):
            parts2[pl.ds(pl.multiple_of(h * NB, NB), NB), p * BLK:(p + 1) * BLK] = x

        @pl.when(k > 0)
        def _():
            finish_u(alpha_old)
        su = total_of(u[...] * u[...])
        swap.wait_recv()
        for p, x in enumerate(split3(core_dst[k])):
            parts2[pl.ds(pl.multiple_of((1 - h) * NB, NB), NB), p * BLK:(p + 1) * BLK] = x
        dense = join3(jnp.dot(put_cols[...], parts2[...], preferred_element_type=F32))
        for j in range(N_CHIP):
            rs_src[k, j, 0:16, :] = dense[j * 16:(j + 1) * 16, :]
            rs_src[k, j, 16:PIECE, :] = su
        for d in CHIPS:
            pltpu.make_async_remote_copy(
                src_ref=rs_src.at[k, chip_at(*d)], dst_ref=rs_dst.at[k, q], send_sem=rs_send.at[k], recv_sem=rs_recv.at[k],
                device_id=row_peer(*d, 0), device_id_type=MESH).start()
        rs_dst[k, q] = rs_src[k, q]
        rhobar, phibar = lsqr(k, rhobar, phibar, alpha_old, beta_old)
        v[...] = v[...] * (1.0 / alpha_old)

        @pl.when(k == 0)
        def _():
            make_put_rows()
        wait_bytes(rs_dst.at[k, pl.ds(0, N_CHIP - 1)], rs_recv.at[k])
        piece = rs_dst[k, 0]
        for j in range(1, N_CHIP):
            piece = piece + rs_dst[k, j]
        vb[k, q, h] = piece[0:16, :]
        for d in CHIPS:
            pltpu.make_async_remote_copy(
                src_ref=vb.at[k, q, h], dst_ref=vb.at[k, q, h], send_sem=ag_send.at[k], recv_sem=ag_recv.at[k],
                device_id=row_peer(*d, 0), device_id_type=MESH).start()
        half_src[k] = piece[16:17, :]
        norm = pltpu.make_async_remote_copy(
            src_ref=half_src.at[k], dst_ref=half_dst.at[k], send_sem=norm_send.at[k], recv_sem=norm_recv.at[k],
            device_id=partner, device_id_type=MESH)
        norm.start()
        norm.wait_recv()
        beta = jnp.sqrt(half_src[k] + half_dst[k])
        inv_beta = 1.0 / beta
        u[...] = u[...] * inv_beta
        u_picks[...] = u_picks[...] * inv_beta
        beta_first = jnp.where(k == 0, beta, beta_first)
        wait_bytes(vb.at[k, pl.ds(0, N_CHIP - 1), h], ag_recv.at[k])
        give = pltpu.make_async_remote_copy(
            src_ref=vb.at[k, :, h], dst_ref=vb.at[k, :, h], send_sem=half_send.at[k], recv_sem=half_recv.at[k],
            device_id=partner, device_id_type=MESH)
        give.start()

        def half_v(s):
            squares = jnp.zeros((16, BLK), F32)
            for j in range(N_CHIP):
                at = pl.ds(pl.multiple_of(j * 32 + s * 16, 16), 16)
                x = vb[k, j, s] * inv_beta - beta * v[at, :]
                v[at, :] = x
                squares = squares + x * x
            return total_of(squares)
        sv = half_v(h)
        give.wait_recv()
        sv = sv + half_v(1 - h)

        for n in range(NB):
            picks[n:n + 1, :] = v[pl.ds(cols_at[0, n], 1), :]
        chosen = picks[...]
        x = jnp.concatenate([chosen, chosen], axis=0).T

        def front(g, _):
            for t in range(UNROLL):
                i = g * UNROLL + t
                sums[pl.ds(pl.multiple_of(i * 8, 8), 8), :] = jnp.sum((tiles[i] * x).reshape(16, 8, BLK), axis=0)
            return 0
        lax.fori_loop(0, NB // UNROLL, front, 0)
        rows = sums[pl.ds(0, NB, stride=8), :]
        for s in range(1, 8):
            rows = rows + sums[pl.ds(s, NB, stride=8), :]
        rows = jnp.concatenate([rows, rows], axis=0).T
        col_src[k + 1, 0:NB, :] = jnp.where(low_half, rows[0:NB, :], rows[NB:BLK, :])
        col_src[k + 1, NB:MSG, :] = sv
        col_start(k + 1)
        col_dst[k + 1, c] = col_src[k + 1]

        def scatter(g):
            for j in range(4):
                for p, x in enumerate(split3(col_dst[k + 1, g * 4 + j, 0:NB, :])):
                    parts[g, j * NB:(j + 1) * NB, p * BLK:(p + 1) * BLK] = x
            return join3(jnp.dot(pick_rows[g], parts[g], preferred_element_type=F32))
        wait_bytes(col_dst.at[k + 1, pl.ds(0, 3)], near_recv.at[k + 1])
        near = scatter(side)
        near_sum[...] = join3(jnp.dot(put_rows[side], parts[side], preferred_element_type=F32))
        wait_bytes(col_dst.at[k + 1, pl.ds(0, 4)], far_recv.at[k + 1])
        far = scatter(1 - side)
        square = col_dst[k + 1, 0, NB:MSG, :]
        for j in range(1, N_COL):
            square = square + col_dst[k + 1, j, NB:MSG, :]
        alpha = jnp.sqrt(square)
        u_picks[...] = (near + far) * (1.0 / alpha) - alpha * u_picks[...]
        return rhobar, phibar, beta_first, alpha, beta

    one = start[0:1, :]
    rhobar, phibar, beta_first, alpha, beta = lax.fori_loop(0, ITERS, step, (one, start[1:2, :], one, one, one))

    finish_u(alpha)
    su = total_of(u[...] * u[...])
    fin_src[...] = su
    for d in CORES:
        pltpu.make_async_remote_copy(
            src_ref=fin_src, dst_ref=fin_dst.at[r], send_sem=fin_send, recv_sem=fin_recv,
            device_id=row_peer(*d), device_id_type=MESH).start()
    fin_dst[r] = su
    rhobar, phibar = lsqr(ITERS, rhobar, phibar, alpha, beta)
    last = fin_dst.at[pl.ds(0, N_ROW - 1)]

    def drain(k, _):
        wait_bytes(core_dst.at[k], core_send.at[k])
        wait_bytes(half_dst.at[k], norm_send.at[k])
        wait_bytes(rs_dst.at[k, pl.ds(0, N_CHIP - 1)], rs_send.at[k])
        wait_bytes(vb.at[k, pl.ds(0, N_CHIP - 1), h], ag_send.at[k])
        wait_bytes(vb.at[k, :, h], half_send.at[k])
        wait_bytes(col_dst.at[k, pl.ds(0, N_COL - 1)], col_send.at[k])
        return 0
    lax.fori_loop(0, ITERS, drain, 0)
    wait_bytes(col_dst.at[ITERS, pl.ds(0, N_COL - 1)], col_send.at[ITERS])
    ids_copy.wait_send()

    wait_bytes(last, fin_recv)
    square = fin_dst[0]
    for j in range(1, N_ROW):
        square = square + fin_dst[j]
    beta = jnp.sqrt(square)
    rho = jnp.sqrt(rhobar * rhobar + beta * beta)
    phi = rhobar / rho * phibar
    sol_out[...] = sol[...] + phi / rho * w[...]
    rel_out[...] = jnp.broadcast_to(beta / rho * phibar / beta_first, (8, BLK))
    wait_bytes(last, fin_send)


def on_device(rhs, blocks, blk_row, blk_col):
    vmem = pl.BlockSpec(memory_space=pltpu.VMEM)
    hbm = pl.BlockSpec(memory_space=pl.ANY)
    dma = pltpu.SemaphoreType.DMA
    many = dma((ITERS + 1,))
    sol, rel = pl.pallas_call(
        kernel,
        out_shape=(pltpu.VMEM((16, BLK), F32), pltpu.VMEM((8, BLK), F32)),
        in_specs=[hbm, hbm, hbm, hbm],
        out_specs=(vmem, vmem),
        scratch_shapes=[
            pltpu.VMEM((NB * BLK, BLK), F32),
            pltpu.VMEM((NB, BLK, BLK), F32),
            pltpu.VMEM((ROWB, BLK), F32),
            pltpu.VMEM((COLB, BLK), F32),
            pltpu.VMEM((NB, BLK), F32),
            pltpu.VMEM((NB, BLK), F32),
            pltpu.VMEM((ROWB, BLK), F32),
            pltpu.VMEM((NB, BLK), F32),
            pltpu.VMEM((NB * 8, BLK), F32),
            pltpu.VMEM((2, ROWB, 256), BF16),
            pltpu.VMEM((2, NB, 256), BF16),
            pltpu.VMEM((256, BLK), BF16),
            pltpu.VMEM((2, 256, 3 * BLK), BF16),
            pltpu.VMEM((2 * NB, 3 * BLK), BF16),
            pltpu.VMEM((ITERS + 1, MSG, BLK), F32),
            pltpu.VMEM((ITERS + 1, N_COL, MSG, BLK), F32),
            pltpu.VMEM((ITERS, NB, BLK), F32),
            pltpu.VMEM((ITERS, NB, BLK), F32),
            pltpu.VMEM((ITERS, N_CHIP, PIECE, BLK), F32),
            pltpu.VMEM((ITERS, N_CHIP, PIECE, BLK), F32),
            pltpu.VMEM((ITERS, 1, BLK), F32),
            pltpu.VMEM((ITERS, 1, BLK), F32),
            pltpu.VMEM((ITERS, N_CHIP, 2, 16, BLK), F32),
            pltpu.VMEM((1, BLK), F32),
            pltpu.VMEM((1, BLK), F32),
            pltpu.VMEM((1, BLK), F32),
            pltpu.VMEM((N_ROW, 1, BLK), F32),
            pltpu.VMEM((16, BLK), F32),
            pltpu.VMEM((16, BLK), F32),
            pltpu.VMEM((8, BLK), F32),
            pltpu.VMEM((1, NB), jnp.int32),
            pltpu.VMEM((1, NB), jnp.int32),
            pltpu.SMEM((1, NB), jnp.int32),
            pltpu.SMEM((1, NB), jnp.int32),
            dma((6,)), many, many, many, many, many, many, many, many, many, many, many, many, many, dma, dma, dma, dma,
        ],
        compiler_params=pltpu.CompilerParams(
            collective_id=0, has_side_effects=True, vmem_limit_bytes=60 * 1024 * 1024),
    )(blk_row.reshape(1, NB), blk_col.reshape(1, NB), rhs.reshape(PER_COL, BLK), blocks.reshape(NB * BLK, BLK))
    return sol.reshape(16 * BLK), rel[0, 0]


def solution(mesh):
    return jax.shard_map(
        on_device,
        mesh=mesh,
        in_specs=(
            P(("row", "col")),
            P("row", "col", None, None, None),
            P("row", "col", None),
            P("row", "col", None),
        ),
        out_specs=(P(("col", "row")), P()),
        check_vma=False,
    )
```

```python
import jax
import jax.numpy as jnp
from jax import lax
from jax.experimental import pallas as pl
from jax.experimental.pallas import tpu as pltpu
from jax.sharding import PartitionSpec as P

BLK = 128
NB = 64
ITERS = 3
N_ROW = 32
N_COL = 8
N_CHIP = 16
ROWB = 496
COLB = 512
PER_COL = 62
MESH = pl.DeviceIdType.MESH
F32 = jnp.float32
BF16 = jnp.bfloat16
MSG = NB + 1
PIECE = 17
UNROLL = 8


def ring(d, n):
    return min(d % n, n - d % n)


CHIPS = sorted(((x, z) for x in range(2) for z in range(8) if (x, z) != (0, 0)), key=lambda t: -(t[0] + ring(t[1], 8)))
CORES = sorted(
    ((x, z, s) for x in range(2) for z in range(8) for s in range(2) if (x, z, s) != (0, 0, 0)),
    key=lambda t: -(t[0] + ring(t[1], 8) + 0.1 * t[2]))
COLS = sorted(((x, y) for x in range(2) for y in range(4) if (x, y) != (0, 0)), key=lambda t: -(4 * t[0] + ring(t[1], 4)))


def split3(x):
    hi = x.astype(BF16)
    rest = x - hi.astype(F32)
    mid = rest.astype(BF16)
    low = (rest - mid.astype(F32)).astype(BF16)
    return hi, mid, low


def join3(x):
    return x[:, 0:BLK] + x[:, BLK:2 * BLK] + x[:, 2 * BLK:3 * BLK]


def total_of(x):
    return jnp.broadcast_to(jnp.sum(jnp.sum(x, axis=0, keepdims=True), axis=1, keepdims=True), (1, BLK))


def kernel(rows_hbm, cols_hbm, rhs_hbm, blocks_hbm, sol_out, rel_out,
           raw, tiles, u, v, picks, spread, sums, put_rows, put_cols, parts, parts2,
           col_src, col_dst, core_src, core_dst, rs_src, rs_dst, vb, ids_src, ids_dst, fin_src, fin_dst, w, sol, start,
           rows_v, cols_v, rows_at, cols_at,
           load_sem, col_send, near_recv, far_recv, core_send, core_recv, rs_send, rs_recv, ag_send, ag_recv,
           half_send, half_recv, ids_send, ids_recv, fin_send, fin_recv):
    r = lax.axis_index("row")
    c = lax.axis_index("col")
    q = r // 2
    h = lax.rem(r, 2)
    x_low = q // 8
    z = lax.rem(q, 8)
    side = c // 4
    y = lax.rem(c, 4)
    partner = {"row": q * 2 + (1 - h), "col": c}

    def chip_at(dx, dz):
        return lax.rem(x_low + dx, 2) * 8 + lax.rem(z + dz, 8)

    def row_peer(dx, dz, dh):
        return {"row": chip_at(dx, dz) * 2 + lax.rem(h + dh, 2), "col": c}

    def col_peer(dx, dy):
        return {"row": r, "col": lax.rem(side + dx, 2) * 4 + lax.rem(y + dy, 4)}

    loads = [
        pltpu.make_async_copy(rows_hbm, rows_v, load_sem.at[0]),
        pltpu.make_async_copy(cols_hbm, cols_v, load_sem.at[1]),
        pltpu.make_async_copy(rhs_hbm, col_src.at[0, pl.ds(0, PER_COL)], load_sem.at[2]),
        pltpu.make_async_copy(rows_hbm, rows_at, load_sem.at[3]),
        pltpu.make_async_copy(cols_hbm, cols_at, load_sem.at[4]),
        pltpu.make_async_copy(blocks_hbm, raw, load_sem.at[5]),
    ]
    for copy in loads:
        copy.start()
    barrier = pltpu.get_barrier_semaphore()
    for d in CORES:
        pl.semaphore_signal(barrier, inc=1, device_id=row_peer(*d), device_id_type=MESH)
    for d in COLS:
        pl.semaphore_signal(barrier, inc=1, device_id=col_peer(*d), device_id_type=MESH)
    col_src[0, PER_COL:MSG, :] = jnp.zeros((MSG - PER_COL, BLK), F32)
    ids_src[...] = jnp.zeros((1, BLK), F32)
    loads[0].wait()
    loads[1].wait()
    col_src[0, NB:MSG, 0:NB] = rows_v[...].astype(F32)
    ids_src[:, 0:NB] = cols_v[...].astype(F32)
    loads[2].wait()
    pl.semaphore_wait(barrier, len(CORES) + len(COLS))

    def col_start(k):
        for d in COLS:
            pltpu.make_async_remote_copy(
                src_ref=col_src.at[k], dst_ref=col_dst.at[k, c], send_sem=col_send.at[k],
                recv_sem=(far_recv if d[0] else near_recv).at[k],
                device_id=col_peer(*d), device_id_type=MESH).start()

    def wait_bytes(ref, sem):
        pltpu.make_async_copy(ref, ref, sem).wait()

    ids_copy = pltpu.make_async_remote_copy(
        src_ref=ids_src, dst_ref=ids_dst, send_sem=ids_send, recv_sem=ids_recv, device_id=partner, device_id_type=MESH)
    col_start(0)
    ids_copy.start()

    lane1 = lax.broadcasted_iota(jnp.int32, (1, BLK), 1)
    low_half = lane1 < NB

    v[...] = jnp.zeros((COLB, BLK), F32)
    start[0:1, :] = jnp.ones((1, BLK), F32)
    start[1:2, :] = jnp.zeros((1, BLK), F32)
    w[...] = jnp.zeros((16, BLK), F32)
    sol[...] = jnp.zeros((16, BLK), F32)
    col_dst[0, c] = col_src[0]
    loads[3].wait()
    loads[4].wait()
    loads[5].wait()

    def arrange(g, _):
        for t in range(2):
            i = g * 2 + t
            top = raw[pl.ds(i, NB, stride=BLK), :]
            low = raw[pl.ds(NB + i, NB, stride=BLK), :]
            tiles[i] = jnp.concatenate([top, low], axis=0).T
        return 0
    lax.fori_loop(0, NB // 2, arrange, 0)

    ids_copy.wait_recv()
    mine = ids_src[...]
    theirs = ids_dst[...]
    first = jnp.where(h == 0, mine, theirs)
    second = jnp.where(h == 0, theirs, mine)
    pair_cols = jnp.where(low_half, first, pltpu.roll(second, NB, 1))
    i256 = lax.broadcasted_iota(jnp.int32, (256, BLK), 0)
    owner_block = ((i256 // 16) * 32 + h * 16 + lax.rem(i256, 16)).astype(F32)
    put_cols[...] = jnp.where(owner_block == pair_cols, 1.0, 0.0).astype(BF16)

    wait_bytes(col_dst.at[0, pl.ds(0, 3)], near_recv.at[0])
    wait_bytes(col_dst.at[0, pl.ds(0, 4)], far_recv.at[0])
    for j in range(N_COL):
        u[j * PER_COL:(j + 1) * PER_COL, :] = col_dst[0, j, 0:PER_COL, :]
    row_number = lax.broadcasted_iota(jnp.int32, (ROWB, BLK), 0).astype(F32)

    def make_put_rows():
        for j in range(N_COL // 2):
            a = col_dst[0, 2 * j, NB:MSG, :]
            b = col_dst[0, 2 * j + 1, NB:MSG, :]
            pair = jnp.where(low_half, a, pltpu.roll(b, NB, 1))
            put_rows[j // 2, :, (j % 2) * BLK:(j % 2 + 1) * BLK] = jnp.where(row_number == pair, 1.0, 0.0).astype(BF16)

    def lsqr(k, rhobar, phibar, alpha, beta):
        unit = v[pl.ds(pl.multiple_of(r * 16, 16), 16), :] / alpha
        rho = jnp.sqrt(rhobar * rhobar + beta * beta)
        cosine = rhobar / rho
        sine = beta / rho
        theta = sine * alpha
        phi = cosine * phibar
        w_now = w[...]
        sol[...] = sol[...] + phi / rho * w_now
        w[...] = unit - theta / rho * w_now
        return jnp.where(k == 1, alpha, -cosine * alpha), jnp.where(k == 1, beta, sine * phibar)

    def step(k, carry):
        rhobar, phibar, beta_first, alpha_old, beta_old = carry
        su = total_of(u[...] * u[...])
        for n in range(NB):
            picks[n:n + 1, :] = u[pl.ds(rows_at[0, n], 1), :]
        chosen = picks[...]
        spread[...] = jnp.concatenate([chosen, pltpu.roll(chosen, NB, 1)], axis=0).T[0:NB, :]

        def back(g, acc):
            for t in range(UNROLL):
                i = g * UNROLL + t
                acc = acc + tiles[i] * spread[pl.ds(i, 1), :]
            return acc
        acc = lax.fori_loop(0, NB // UNROLL, back, jnp.zeros((BLK, BLK), F32)).T
        core_src[k, 0:NB, :] = acc[0:NB, :] + acc[NB:BLK, :]
        core_src[k, NB:MSG, :] = su
        swap = pltpu.make_async_remote_copy(
            src_ref=core_src.at[k], dst_ref=core_dst.at[k], send_sem=core_send.at[k], recv_sem=core_recv.at[k],
            device_id=partner, device_id_type=MESH)
        swap.start()
        for p, x in enumerate(split3(core_src[k, 0:NB, :])):
            parts2[pl.ds(pl.multiple_of(h * NB, NB), NB), p * BLK:(p + 1) * BLK] = x
        swap.wait_recv()
        for p, x in enumerate(split3(core_dst[k, 0:NB, :])):
            parts2[pl.ds(pl.multiple_of((1 - h) * NB, NB), NB), p * BLK:(p + 1) * BLK] = x
        dense = join3(jnp.dot(put_cols[...], parts2[...], preferred_element_type=F32))
        both = su + core_dst[k, NB:MSG, :]
        for j in range(N_CHIP):
            rs_src[k, j, 0:16, :] = dense[j * 16:(j + 1) * 16, :]
            rs_src[k, j, 16:PIECE, :] = both
        for d in CHIPS:
            pltpu.make_async_remote_copy(
                src_ref=rs_src.at[k, chip_at(*d)], dst_ref=rs_dst.at[k, q], send_sem=rs_send.at[k], recv_sem=rs_recv.at[k],
                device_id=row_peer(*d, 0), device_id_type=MESH).start()
        rs_dst[k, q] = rs_src[k, q]
        rhobar, phibar = lsqr(k, rhobar, phibar, alpha_old, beta_old)
        v[...] = v[...] * (1.0 / alpha_old)

        @pl.when(k == 0)
        def _():
            make_put_rows()
        wait_bytes(rs_dst.at[k, pl.ds(0, N_CHIP - 1)], rs_recv.at[k])
        piece = rs_dst[k, 0]
        for j in range(1, N_CHIP):
            piece = piece + rs_dst[k, j]
        vb[k, q, h] = piece[0:16, :]
        for d in CHIPS:
            pltpu.make_async_remote_copy(
                src_ref=vb.at[k, q, h], dst_ref=vb.at[k, q, h], send_sem=ag_send.at[k], recv_sem=ag_recv.at[k],
                device_id=row_peer(*d, 0), device_id_type=MESH).start()
        beta = jnp.sqrt(piece[16:17, :])
        inv_beta = 1.0 / beta
        u[...] = u[...] * inv_beta
        beta_first = jnp.where(k == 0, beta, beta_first)
        wait_bytes(vb.at[k, pl.ds(0, N_CHIP - 1), h], ag_recv.at[k])
        give = pltpu.make_async_remote_copy(
            src_ref=vb.at[k, :, h], dst_ref=vb.at[k, :, h], send_sem=half_send.at[k], recv_sem=half_recv.at[k],
            device_id=partner, device_id_type=MESH)
        give.start()

        def half_v(s):
            squares = jnp.zeros((16, BLK), F32)
            for j in range(N_CHIP):
                at = pl.ds(pl.multiple_of(j * 32 + s * 16, 16), 16)
                x = vb[k, j, s] * inv_beta - beta * v[at, :]
                v[at, :] = x
                squares = squares + x * x
            return total_of(squares)
        sv = half_v(h)
        give.wait_recv()
        sv = sv + half_v(1 - h)

        for n in range(NB):
            picks[n:n + 1, :] = v[pl.ds(cols_at[0, n], 1), :]
        chosen = picks[...]
        x = jnp.concatenate([chosen, chosen], axis=0).T

        def front(g, _):
            for t in range(UNROLL):
                i = g * UNROLL + t
                sums[pl.ds(pl.multiple_of(i * 8, 8), 8), :] = jnp.sum((tiles[i] * x).reshape(16, 8, BLK), axis=0)
            return 0
        lax.fori_loop(0, NB // UNROLL, front, 0)
        rows = sums[pl.ds(0, NB, stride=8), :]
        for s in range(1, 8):
            rows = rows + sums[pl.ds(s, NB, stride=8), :]
        rows = jnp.concatenate([rows, rows], axis=0).T
        col_src[k + 1, 0:NB, :] = jnp.where(low_half, rows[0:NB, :], rows[NB:BLK, :])
        col_src[k + 1, NB:MSG, :] = sv
        col_start(k + 1)
        col_dst[k + 1, c] = col_src[k + 1]

        def scatter(g):
            for j in range(4):
                for p, x in enumerate(split3(col_dst[k + 1, g * 4 + j, 0:NB, :])):
                    parts[g, j * NB:(j + 1) * NB, p * BLK:(p + 1) * BLK] = x
            return join3(jnp.dot(put_rows[g], parts[g], preferred_element_type=F32))
        wait_bytes(col_dst.at[k + 1, pl.ds(0, 3)], near_recv.at[k + 1])
        near = scatter(side)
        wait_bytes(col_dst.at[k + 1, pl.ds(0, 4)], far_recv.at[k + 1])
        far = scatter(1 - side)
        square = col_dst[k + 1, 0, NB:MSG, :]
        for j in range(1, N_COL):
            square = square + col_dst[k + 1, j, NB:MSG, :]
        alpha = jnp.sqrt(square)
        u[...] = (near + far) * (1.0 / alpha) - alpha * u[...]
        return rhobar, phibar, beta_first, alpha, beta

    one = start[0:1, :]
    rhobar, phibar, beta_first, alpha, beta = lax.fori_loop(0, ITERS, step, (one, start[1:2, :], one, one, one))

    su = total_of(u[...] * u[...])
    fin_src[...] = su
    for d in CORES:
        pltpu.make_async_remote_copy(
            src_ref=fin_src, dst_ref=fin_dst.at[r], send_sem=fin_send, recv_sem=fin_recv,
            device_id=row_peer(*d), device_id_type=MESH).start()
    fin_dst[r] = su
    rhobar, phibar = lsqr(ITERS, rhobar, phibar, alpha, beta)
    last = fin_dst.at[pl.ds(0, N_ROW - 1)]

    def drain(k, _):
        wait_bytes(core_dst.at[k], core_send.at[k])
        wait_bytes(rs_dst.at[k, pl.ds(0, N_CHIP - 1)], rs_send.at[k])
        wait_bytes(vb.at[k, pl.ds(0, N_CHIP - 1), h], ag_send.at[k])
        wait_bytes(vb.at[k, :, h], half_send.at[k])
        wait_bytes(col_dst.at[k, pl.ds(0, N_COL - 1)], col_send.at[k])
        return 0
    lax.fori_loop(0, ITERS, drain, 0)
    wait_bytes(col_dst.at[ITERS, pl.ds(0, N_COL - 1)], col_send.at[ITERS])
    ids_copy.wait_send()

    wait_bytes(last, fin_recv)
    square = fin_dst[0]
    for j in range(1, N_ROW):
        square = square + fin_dst[j]
    beta = jnp.sqrt(square)
    rho = jnp.sqrt(rhobar * rhobar + beta * beta)
    phi = rhobar / rho * phibar
    sol_out[...] = sol[...] + phi / rho * w[...]
    rel_out[...] = jnp.broadcast_to(beta / rho * phibar / beta_first, (8, BLK))
    wait_bytes(last, fin_send)


def on_device(rhs, blocks, blk_row, blk_col):
    vmem = pl.BlockSpec(memory_space=pltpu.VMEM)
    hbm = pl.BlockSpec(memory_space=pl.ANY)
    dma = pltpu.SemaphoreType.DMA
    many = dma((ITERS + 1,))
    sol, rel = pl.pallas_call(
        kernel,
        out_shape=(pltpu.VMEM((16, BLK), F32), pltpu.VMEM((8, BLK), F32)),
        in_specs=[hbm, hbm, hbm, hbm],
        out_specs=(vmem, vmem),
        scratch_shapes=[
            pltpu.VMEM((NB * BLK, BLK), F32),
            pltpu.VMEM((NB, BLK, BLK), F32),
            pltpu.VMEM((ROWB, BLK), F32),
            pltpu.VMEM((COLB, BLK), F32),
            pltpu.VMEM((NB, BLK), F32),
            pltpu.VMEM((NB, BLK), F32),
            pltpu.VMEM((NB * 8, BLK), F32),
            pltpu.VMEM((2, ROWB, 256), BF16),
            pltpu.VMEM((256, BLK), BF16),
            pltpu.VMEM((2, 256, 3 * BLK), BF16),
            pltpu.VMEM((2 * NB, 3 * BLK), BF16),
            pltpu.VMEM((ITERS + 1, MSG, BLK), F32),
            pltpu.VMEM((ITERS + 1, N_COL, MSG, BLK), F32),
            pltpu.VMEM((ITERS, MSG, BLK), F32),
            pltpu.VMEM((ITERS, MSG, BLK), F32),
            pltpu.VMEM((ITERS, N_CHIP, PIECE, BLK), F32),
            pltpu.VMEM((ITERS, N_CHIP, PIECE, BLK), F32),
            pltpu.VMEM((ITERS, N_CHIP, 2, 16, BLK), F32),
            pltpu.VMEM((1, BLK), F32),
            pltpu.VMEM((1, BLK), F32),
            pltpu.VMEM((1, BLK), F32),
            pltpu.VMEM((N_ROW, 1, BLK), F32),
            pltpu.VMEM((16, BLK), F32),
            pltpu.VMEM((16, BLK), F32),
            pltpu.VMEM((8, BLK), F32),
            pltpu.VMEM((1, NB), jnp.int32),
            pltpu.VMEM((1, NB), jnp.int32),
            pltpu.SMEM((1, NB), jnp.int32),
            pltpu.SMEM((1, NB), jnp.int32),
            dma((6,)), many, many, many, many, many, many, many, many, many, many, many, dma, dma, dma, dma,
        ],
        compiler_params=pltpu.CompilerParams(
            collective_id=0, has_side_effects=True, vmem_limit_bytes=60 * 1024 * 1024),
    )(blk_row.reshape(1, NB), blk_col.reshape(1, NB), rhs.reshape(PER_COL, BLK), blocks.reshape(NB * BLK, BLK))
    return sol.reshape(16 * BLK), rel[0, 0]


def solution(mesh):
    return jax.shard_map(
        on_device,
        mesh=mesh,
        in_specs=(
            P(("row", "col")),
            P("row", "col", None, None, None),
            P("row", "col", None),
            P("row", "col", None),
        ),
        out_specs=(P(("col", "row")), P()),
        check_vma=False,
    )
```
